32 devices in a mesh: seq: 8 (over y, x, core), head: 4 (over z).
Axes of the slice: x: 2, y: 2, z: 4, core: 2. Of those that a mesh axis runs over, the one named last changes fastest.
Arguments:
- query_rows: bfloat16 [8192, 2048], P(('seq', 'head')), may hold values from -1.796875 to 1.796875
- key_rows: bfloat16 [8192, 2048], P(('seq', 'head')), may hold values from -1.796875 to 1.796875
- value_rows: bfloat16 [8192, 2048], P(('seq', 'head')), may hold values from -1.796875 to 1.796875
- out_grad: bfloat16 [8192, 2048], P(('seq', 'head')), may hold values from -1.796875 to 1.796875
- decay: float32 [16, 8192], P('head', 'seq'), may hold values from 0 to 2
Outputs:
- attended: bfloat16 [8192, 2048], P(('seq', 'head'))
- query_grad: bfloat16 [8192, 2048], P(('seq', 'head'))
- key_grad: bfloat16 [8192, 2048], P(('seq', 'head'))
- value_grad: bfloat16 [8192, 2048], P(('seq', 'head'))
The draws below stay inside these ranges and needn't reach their ends.
All inputs are finite; a program needn't handle non-finite values.
Results may differ from the reference program's by a relative error of at most 0.0083.
Values may be sent and summed in bfloat16 or wider, within the bound.
No kernel may reach another device: no remote copies, remote signals or barrier semaphores. Data moves between devices by JAX's collectives and lax.ppermute only.
A program may use at most 128 MiB of HBM per device.

```python
import jax
import jax.numpy as jnp
from jax import lax

E = 128
BLOCK = 1024
HEAD_COUNT = 16
SEQUENCE_TOKENS = 8192
N_SEQ = 8


def draw_decay(key, part):
    random_subkeys = jax.random.split(key, 8)
    quick_share = 0.25
    middle_share = 0.25
    slow_low = 0.3
    head_draw = jax.random.uniform(random_subkeys[0], (HEAD_COUNT,))
    quick_heads = head_draw < quick_share
    middle_heads = jnp.logical_and(head_draw >= quick_share, head_draw < quick_share + middle_share)
    quick_rate = jnp.exp(jax.random.uniform(random_subkeys[1], (HEAD_COUNT,), minval=jnp.log(0.015), maxval=jnp.log(0.04)))
    middle_rate = jnp.exp(jax.random.uniform(random_subkeys[7], (HEAD_COUNT,), minval=jnp.log(0.15), maxval=0.0)) / BLOCK
    slow_rate = jnp.exp(jax.random.uniform(random_subkeys[2], (HEAD_COUNT,), minval=jnp.log(slow_low), maxval=jnp.log(0.9))) / SEQUENCE_TOKENS
    baseline_rate = jnp.where(quick_heads, quick_rate, jnp.where(middle_heads, middle_rate, slow_rate))
    blocks = SEQUENCE_TOKENS // BLOCK
    block_multiplier = jnp.exp(jax.random.uniform(random_subkeys[3], (HEAD_COUNT, blocks), minval=jnp.log(0.5), maxval=jnp.log(2.0)))
    block_multiplier = jnp.repeat(block_multiplier, BLOCK, axis=1)
    token_multiplier = jax.random.uniform(random_subkeys[4], (HEAD_COUNT, SEQUENCE_TOKENS), minval=0.5, maxval=1.5)
    spike_locations = jax.random.randint(random_subkeys[5], (HEAD_COUNT, 2), 0, SEQUENCE_TOKENS)
    spike_loss = jax.random.uniform(random_subkeys[6], (HEAD_COUNT, 2), minval=0.22, maxval=0.69)
    token_positions = jnp.arange(SEQUENCE_TOKENS)
    spike_events = jnp.sum(jnp.where(token_positions[None, None, :] == spike_locations[:, :, None], spike_loss[:, :, None], 0.0), axis=1)
    return (baseline_rate[:, None] * block_multiplier * token_multiplier + spike_events).astype(jnp.float32)


def block_scale(key, shape, shards, low, top_value):
    def one(axis_at, blocks):
        steps = jax.random.uniform(jax.random.fold_in(jax.random.fold_in(key, 6), axis_at), (blocks,), jnp.float32, low / len(shards), top_value / len(shards))
        return jnp.repeat(jnp.exp(steps), shape[axis_at] // blocks).reshape((-1,) + (1,) * (len(shape) - axis_at - 1))

    loudness = one(*shards[0])
    for cut in shards[1:]:
        loudness = loudness * one(*cut)
    return loudness


def gaussian(stream_key, dims, spread, limit, pieces=(), held_as=jnp.bfloat16):
    entries = jax.random.normal(stream_key, dims, jnp.float32) * spread
    if len(pieces) > 0:
        entries = block_scale(stream_key, dims, pieces, -0.22, 0.18) * entries
    return jnp.clip(entries, min=-limit, max=limit).astype(held_as)


def setup_inputs(seed: int = 0) -> dict:
    key_list = jax.random.split(jax.random.key(seed), 6)
    query_rows = gaussian(key_list[0], (SEQUENCE_TOKENS, HEAD_COUNT * E), 0.3, 1.796875, ((0, 32),))
    key_rows = gaussian(key_list[1], (SEQUENCE_TOKENS, HEAD_COUNT * E), 0.3, 1.796875, ((0, 32),))
    value_rows = gaussian(key_list[2], (SEQUENCE_TOKENS, HEAD_COUNT * E), 0.3, 1.796875, ((0, 32),))
    out_grad = gaussian(key_list[3], (SEQUENCE_TOKENS, HEAD_COUNT * E), 0.3, 1.796875, ((0, 32),))
    decay = draw_decay(jax.random.fold_in(key_list[5], 71), 0)
    return {"query_rows": query_rows, "key_rows": key_rows, "value_rows": value_rows, "out_grad": out_grad, "decay": decay}


def rounded(values):
    return lax.optimization_barrier(values.astype(jnp.bfloat16)).astype(jnp.float32)


def rows_by_block(array):
    return array.reshape(N_SEQ, BLOCK, HEAD_COUNT, E).transpose(0, 2, 1, 3)


def block_summary(items):
    query_part, key_part, value_part, grad_part, decay_rates = items
    scale_factor = E ** -0.5
    running = jnp.cumsum(decay_rates, axis=1)
    block_log = running[:, -1]
    weights = jnp.exp(-(block_log[:, None] - running))
    growth = jnp.exp(-running)
    keyed = rounded(key_part.astype(jnp.float32) * weights[:, :, None])
    queried = rounded(query_part.astype(jnp.float32) * growth[:, :, None])
    update = jnp.einsum('hcd,hce->hde', keyed, value_part.astype(jnp.float32))
    source = scale_factor * jnp.einsum('hcd,hce->hde', queried, grad_part.astype(jnp.float32))
    return block_log, update, source


def block_result(items):
    query_part, key_part, value_part, grad_part, decay_rates, state_in, state_grad = items
    scale_factor = E ** -0.5
    running = jnp.cumsum(decay_rates, axis=1)
    block_log = running[:, -1]
    weights = jnp.exp(-(block_log[:, None] - running))
    growth = jnp.exp(-running)
    length = decay_rates.shape[1]
    causal = (jnp.arange(length)[:, None] >= jnp.arange(length)[None, :])[None]
    spread_log = running[:, :, None] - running[:, None, :]
    decay_mask = jnp.where(causal, jnp.exp(-jnp.where(causal, spread_log, 0.0)), 0.0)
    query_f = query_part.astype(jnp.float32)
    key_f = key_part.astype(jnp.float32)
    value_f = value_part.astype(jnp.float32)
    grad_f = grad_part.astype(jnp.float32)
    state_half = rounded(state_in)
    grad_half = rounded(state_grad)
    scores = rounded(scale_factor * jnp.einsum('htd,hsd->hts', query_f, key_f) * decay_mask)
    grad_scores = rounded(scale_factor * jnp.einsum('hte,hse->hts', grad_f, value_f) * decay_mask)
    attended = jnp.einsum('hts,hse->hte', scores, value_f) + scale_factor * growth[:, :, None] * jnp.einsum('htd,hde->hte', query_f, state_half)
    query_grad = jnp.einsum('hts,hsd->htd', grad_scores, key_f) + scale_factor * growth[:, :, None] * jnp.einsum('hte,hde->htd', grad_f, state_half)
    key_grad = jnp.einsum('hts,htd->hsd', grad_scores, query_f) + weights[:, :, None] * jnp.einsum('hse,hde->hsd', value_f, grad_half)
    value_grad = jnp.einsum('hts,hte->hse', scores, grad_f) + weights[:, :, None] * jnp.einsum('hsd,hde->hse', key_f, grad_half)
    return (attended.astype(jnp.bfloat16), query_grad.astype(jnp.bfloat16), key_grad.astype(jnp.bfloat16), value_grad.astype(jnp.bfloat16))


def forward_step(state, items):
    block_log, update = items
    return jnp.exp(-block_log)[:, None, None] * state + update, state


def backward_step(state, items):
    block_log, source = items
    return source + jnp.exp(-block_log)[:, None, None] * state, state


def reference(query_rows, key_rows, value_rows, out_grad, decay):
    query_blocks = rows_by_block(query_rows)
    key_blocks = rows_by_block(key_rows)
    value_blocks = rows_by_block(value_rows)
    grad_blocks = rows_by_block(out_grad)
    decay_blocks = decay.reshape(HEAD_COUNT, N_SEQ, BLOCK).transpose(1, 0, 2)
    block_logs, updates, sources = lax.map(block_summary, (query_blocks, key_blocks, value_blocks, grad_blocks, decay_blocks))
    zero_state = jnp.zeros((HEAD_COUNT, E, E), jnp.float32)
    _, states_in = lax.scan(forward_step, zero_state, (block_logs, updates))
    _, states_grad = lax.scan(backward_step, zero_state, (block_logs, sources), reverse=True)
    results = lax.map(block_result, (query_blocks, key_blocks, value_blocks, grad_blocks, decay_blocks, states_in, states_grad))
    merged = tuple(part.transpose(0, 2, 1, 3).reshape(SEQUENCE_TOKENS, HEAD_COUNT * E) for part in results)
    return (merged[0], merged[1], merged[2], merged[3])
```

```python
import functools

import jax
import jax.numpy as jnp
from jax import lax
from jax.experimental import pallas as pl
from jax.experimental.pallas import tpu as pltpu
from jax.sharding import PartitionSpec as P


SEQ = "seq"
HEAD = "head"
PAIR = 2
CHUNKS = 2
F32 = jnp.float32
BF16 = jnp.bfloat16


def dot(a, b, contract, precision=None):
    return lax.dot_general(
        a, b, (((contract[0],), (contract[1],)), ((), ())),
        precision=precision, preferred_element_type=F32,
    )


def params(mib=16):
    return pltpu.CompilerParams(vmem_limit_bytes=mib << 20)


def split(x):
    high = x.astype(BF16)
    rest = x - high.astype(F32)
    middle = rest.astype(BF16)
    return high, middle, (rest - middle.astype(F32)).astype(BF16)


def prepare(place_ref, decay_refs, row_ref, col_ref, log_ref):
    me, seq_at = place_ref[0], place_ref[1]
    owners = len(decay_refs)
    heads, tokens = row_ref.shape[1:]
    at = lax.broadcasted_iota(jnp.int32, (tokens, tokens), 0)
    by = lax.broadcasted_iota(jnp.int32, (tokens, tokens), 1)
    upto = (at <= by).astype(BF16)
    since = (by <= at).astype(BF16)
    start = pl.multiple_of(me * tokens, tokens)
    own = jnp.concatenate([ref[:, pl.ds(start, tokens)] for ref in decay_refs], axis=0)
    pieces = split(own)
    rows = sum(dot(piece, upto, (1, 0)) for piece in pieces)
    cols = sum(dot(since, piece, (1, 1)) for piece in pieces)
    for slot in range(owners):
        row_ref[slot] = rows[slot * heads : (slot + 1) * heads]
        col_ref[slot] = cols[:, slot * heads : (slot + 1) * heads]
    lane = lax.broadcasted_iota(jnp.int32, log_ref.shape, 1)
    logs = jnp.zeros(log_ref.shape, F32)
    for index in range(owners):
        total = jnp.sum(decay_refs[0][:, index * tokens : (index + 1) * tokens], axis=1, keepdims=True)
        logs = logs + jnp.where(lane == seq_at * owners + index, total, 0.0)
    log_ref[...] = logs


def summarize(place_ref, row_ref, col_ref, token_refs, out_refs, chunk, part):
    q_ref, k_ref, v_ref, g_ref = token_refs
    owners = len(out_refs)
    heads, tokens = row_ref.shape[1:]
    width = out_refs[0].shape[-1]
    scale = width ** (-0.5)
    for slot, out_ref in enumerate(out_refs):
        owner = lax.rem(place_ref[0] - slot + owners, owners)
        for member in range(part):
            head = chunk * part + member
            cols = pl.ds(pl.multiple_of((owner * heads + head) * width, width), width)
            col = col_ref[slot][:, head : head + 1]
            last = row_ref[slot][head : head + 1, tokens - 1 : tokens]
            weight = jnp.exp(-(last - col))
            growth = jnp.exp(-col)
            keyed = (k_ref[:, cols].astype(F32) * weight).astype(BF16)
            queried = (q_ref[:, cols].astype(F32) * growth).astype(BF16)
            out_ref[0, member] = dot(keyed, v_ref[:, cols], (0, 0)).astype(BF16)
            out_ref[1, member] = (scale * dot(queried, g_ref[:, cols], (0, 0))).astype(BF16)


def first_kernel(place_ref, *refs, part, owners):
    decay_refs, refs = refs[:owners], refs[owners:]
    token_refs, refs = refs[:4], refs[4:]
    row_ref, col_ref, log_ref = refs[:3]
    prepare(place_ref, decay_refs, row_ref, col_ref, log_ref)
    summarize(place_ref, row_ref, col_ref, token_refs, refs[3:], 0, part)


def later_kernel(place_ref, row_ref, col_ref, *refs, chunk, part):
    summarize(place_ref, row_ref, col_ref, refs[:4], refs[4:], chunk, part)


def link_layout(owners, far):
    sizes = dict(near0=owners * owners, near1=owners * owners, after=owners, before=owners, pair=4, other=2, far0=far, far1=far)
    at, total = {}, 0
    for name, size in sizes.items():
        at[name] = total
        total += size
    return sizes, at, -(-total // 8) * 8


def link_kernel(place_ref, log_ref, w_ref, *, owners, far):
    me, seq_at = place_ref[0], place_ref[1]
    sizes, at, length = link_layout(owners, far)
    heads, places = log_ref.shape
    span, first = owners * PAIR, seq_at * owners
    pair_at = lax.rem(seq_at, PAIR)
    far_at = lax.div(seq_at, PAIR)
    lead = pair_at == 0
    other = seq_at + 1 - 2 * pair_at
    index = lax.broadcasted_iota(jnp.int32, (length, 1), 0)
    low = high = keep = jnp.zeros((length, 1), jnp.int32)

    def put(name, low_, high_, keep_):
        nonlocal low, high, keep
        here = (index >= at[name]) & (index < at[name] + sizes[name])
        low = jnp.where(here, low_, low)
        high = jnp.where(here, high_, high)
        keep = jnp.where(here, jnp.where(keep_, 1, 0), keep)

    for side in range(2):
        r = index - at[f"near{side}"]
        to = first + lax.rem(me + lax.div(r, owners), owners)
        of = first + lax.rem(me + lax.rem(r, owners), owners)
        if side == 0:
            put("near0", of, to, of < to)
        else:
            put("near1", to, of, to < of)
    place = first + lax.rem(me + index - at["after"], owners)
    put("after", place, first + owners, index >= 0)
    place = first + lax.rem(me + index - at["before"], owners)
    put("before", first - 1, place, index >= 0)
    r = index - at["pair"]
    block = jnp.where(lax.rem(r, 2) == 0, other, seq_at)
    leading = jnp.where((r == 0) | (r == 3), 0, 1) == pair_at
    put("pair", block * owners - 1, jnp.where(leading, (block + 1) * owners, 0), index >= 0)
    put("other", 0, 0, jnp.where(index - at["other"] == 0, 1, 0) == pair_at)
    for side in range(2):
        heard = far_at - 1 - (index - at[f"far{side}"])
        source = jnp.where(heard < 0, heard + far + 1, heard)
        if side == 0:
            put("far0", (source + 1) * span - 1, first, heard >= 0)
        else:
            put("far1", first + owners - 1, source * span, heard < 0)
    spot = lax.broadcasted_iota(jnp.int32, (length, places), 1)
    inside = ((spot > low) & (spot < high)).astype(BF16)
    total = sum(dot(inside, piece, (1, 1)) for piece in split(log_ref[...]))
    weight = jnp.where(keep > 0, jnp.exp(-total), 0.0)
    for head in range(heads):
        w_ref[head] = jnp.broadcast_to(weight[:, head : head + 1], w_ref.shape[1:])


def total_kernel(w_ref, *refs, chunk, part, at):
    out_ref = refs[-1]
    for side, name in enumerate(("after", "before")):
        for member in range(part):
            head = chunk * part + member
            total = 0.0
            for slot, ref in enumerate(refs[:-1]):
                index = at[name] + slot
                total = total + w_ref[head, index : index + 1] * ref[side, member].astype(F32)
            out_ref[side, member] = total.astype(BF16)


def pair_kernel(place_ref, w_ref, own_ref, other_ref, *out_refs, chunk, part, at):
    far_at = lax.div(place_ref[1], PAIR)
    for member in range(part):
        head = chunk * part + member
        both = []
        for side in range(2):
            index = at["pair"] + 2 * side
            both.append(
                w_ref[head, index : index + 1] * own_ref[side, member].astype(F32)
                + w_ref[head, index + 1 : index + 2] * other_ref[side, member].astype(F32)
            )
        for slot, out_ref in enumerate(out_refs):
            onward = far_at + slot < len(out_refs)
            out_ref[member] = jnp.where(onward, both[0], both[1]).astype(BF16)


def state_kernel(w_ref, *refs, chunk, part, at, owners, far):
    ins = refs[:owners]
    other_ref = refs[owners]
    far_refs = refs[owners + 1 : owners + 1 + far]
    out_refs = refs[owners + 1 + far :]
    for member in range(part):
        head = chunk * part + member

        def weight(index):
            return w_ref[head, index : index + 1]

        for side, enter in enumerate(("before", "after")):
            base = weight(at["other"] + side) * other_ref[side, member].astype(F32)
            for slot, ref in enumerate(far_refs):
                base = base + weight(at[f"far{side}"] + slot) * ref[member].astype(F32)
            pieces = [ref[side, member].astype(F32) for ref in ins]
            for slot, out_ref in enumerate(out_refs):
                value = weight(at[enter] + slot) * base
                for source, piece in enumerate(pieces):
                    if source != slot:
                        value = value + weight(at[f"near{side}"] + slot * owners + source) * piece
                out_ref[side, member] = value.astype(BF16)


def result_kernel(place_ref, row_ref, col_ref, q_ref, k_ref, v_ref, g_ref, *refs, chunk, part, owners, carried):
    state_refs = refs[:owners]
    refs = refs[owners + carried :]
    att_ref, qg_ref, kg_ref, vg_ref, state = refs
    step = pl.program_id(0)
    width = state.shape[-1]
    scale = width ** (-0.5)
    tokens = q_ref.shape[0]
    for slot, ref in enumerate(state_refs):

        @pl.when(step == slot)
        def _():
            state[...] = ref[...]

    at = lax.broadcasted_iota(jnp.int32, (tokens, tokens), 0)
    by = lax.broadcasted_iota(jnp.int32, (tokens, tokens), 1)
    causal = at >= by
    for member in range(part):
        head = chunk * part + member
        cols = slice(member * width, (member + 1) * width)
        row = row_ref[0][head : head + 1, :]
        col = col_ref[0][:, head : head + 1]
        last = row[:, tokens - 1 : tokens]
        weight = jnp.exp(-(last - col))
        growth = scale * jnp.exp(-col)
        mask = jnp.where(causal, scale * jnp.exp(-jnp.where(causal, col - row, 0.0)), 0.0)
        q, k, v, g = q_ref[:, cols], k_ref[:, cols], v_ref[:, cols], g_ref[:, cols]
        scores = (dot(q, k, (1, 1)) * mask).astype(BF16)
        grads = (dot(g, v, (1, 1)) * mask).astype(BF16)
        ahead = state[0, member]
        back = state[1, member]
        att_ref[:, cols] = (dot(scores, v, (1, 0)) + growth * dot(q, ahead, (1, 0))).astype(BF16)
        qg_ref[:, cols] = (dot(grads, k, (1, 0)) + growth * dot(g, ahead, (1, 1))).astype(BF16)
        kg_ref[:, cols] = (dot(grads, q, (0, 0)) + weight * dot(v, back, (1, 1))).astype(BF16)
        vg_ref[:, cols] = (dot(scores, g, (0, 0)) + weight * dot(k, back, (1, 0))).astype(BF16)


def on_device(query_rows, key_rows, value_rows, out_grad, decay, *, seq_size, owners):
    seq_at = lax.axis_index(SEQ)
    head_at = lax.axis_index(HEAD)
    heads = decay.shape[0]
    tokens, columns = query_rows.shape
    width = columns // (heads * owners)
    chunks = CHUNKS if heads % CHUNKS == 0 else 1
    part = heads // chunks
    far = seq_size // PAIR - 1
    place = jnp.stack([head_at, seq_at]).astype(jnp.int32)
    _, at, table = link_layout(owners, far)

    def along_head(array, shift):
        return lax.ppermute(array, HEAD, [(i, (i + shift) % owners) for i in range(owners)])

    smem = pl.BlockSpec(memory_space=pltpu.SMEM)
    whole = pl.BlockSpec(memory_space=pltpu.VMEM)
    row_shape = jax.ShapeDtypeStruct((owners, heads, tokens), F32)
    col_shape = jax.ShapeDtypeStruct((owners, tokens, heads), F32)
    log_shape = jax.ShapeDtypeStruct((heads, seq_size * owners), F32)
    state_shape = jax.ShapeDtypeStruct((2, part, width, width), BF16)
    inputs = (query_rows, key_rows, value_rows, out_grad)
    cost = pl.CostEstimate(
        flops=4 * tokens * width * width * heads * owners // chunks,
        bytes_accessed=8 * tokens * columns // chunks,
        transcendentals=0,
    )

    decays = [decay] + [along_head(decay, shift) for shift in range(1, owners)]
    rows, cols, logs, *first = pl.pallas_call(
        functools.partial(first_kernel, part=part, owners=owners),
        out_shape=(row_shape, col_shape, log_shape) + (state_shape,) * owners,
        in_specs=[smem] + [whole] * (owners + 4),
        out_specs=(whole,) * (3 + owners),
        cost_estimate=cost,
        compiler_params=params(),
        name="first",
    )(place, *decays, *inputs)
    summaries = [first]
    for chunk in range(1, chunks):
        summaries.append(
            pl.pallas_call(
                functools.partial(later_kernel, chunk=chunk, part=part),
                out_shape=(state_shape,) * owners,
                in_specs=[smem] + [whole] * 6,
                out_specs=(whole,) * owners,
                cost_estimate=cost,
                compiler_params=params(),
                name=f"summary{chunk}",
            )(place, rows, cols, *inputs)
        )

    step = 1
    while step < seq_size:
        logs = logs + lax.ppermute(logs, SEQ, [(i, i ^ step) for i in range(seq_size)])
        step *= 2
    weights = pl.pallas_call(
        functools.partial(link_kernel, owners=owners, far=far),
        out_shape=jax.ShapeDtypeStruct((heads, table, width), F32),
        in_specs=[smem, whole],
        out_specs=whole,
        compiler_params=params(),
        name="link",
    )(place, logs)

    def token_specs(chunk):
        return pl.BlockSpec(
            (tokens, part * width),
            lambda j, place_ref: (0, lax.rem(place_ref[0] - j + owners, owners) * chunks + chunk),
        )

    row_spec = pl.BlockSpec((1, heads, tokens), lambda j, place_ref: (j, 0, 0))
    col_spec = pl.BlockSpec((1, tokens, heads), lambda j, place_ref: (j, 0, 0))
    state_spec = pl.BlockSpec((2, part, width, width), lambda j, place_ref: (0, 0, 0, 0))
    outs = None
    for chunk in range(chunks):
        own = summaries[chunk]
        here = [own[0]] + [along_head(own[shift], -shift) for shift in range(1, owners)]
        total = pl.pallas_call(
            functools.partial(total_kernel, chunk=chunk, part=part, at=at),
            out_shape=state_shape,
            in_specs=[whole] * (owners + 1),
            out_specs=whole,
            compiler_params=params(),
            name=f"total{chunk}",
        )(weights, *here)
        other = lax.ppermute(total, SEQ, [(i, i ^ 1) for i in range(seq_size)])
        far_shape = jax.ShapeDtypeStruct((part, width, width), BF16)
        sent = pl.pallas_call(
            functools.partial(pair_kernel, chunk=chunk, part=part, at=at),
            out_shape=(far_shape,) * far,
            in_specs=[smem, whole, whole, whole],
            out_specs=(whole,) * far,
            compiler_params=params(),
            name=f"pair{chunk}",
        )(place, weights, total, other)
        heard = [
            lax.ppermute(
                array, SEQ, [(i, (i + PAIR * (slot + 1)) % seq_size) for i in range(seq_size)]
            )
            for slot, array in enumerate(sent)
        ]
        states = pl.pallas_call(
            functools.partial(
                state_kernel, chunk=chunk, part=part, at=at, owners=owners, far=far
            ),
            out_shape=(state_shape,) * owners,
            in_specs=[whole] * (owners + far + 2),
            out_specs=(whole,) * owners,
            compiler_params=params(),
            name=f"state{chunk}",
        )(weights, *here, other, *heard)
        states = [states[0]] + [along_head(states[shift], shift) for shift in range(1, owners)]
        carried = 0 if outs is None else 4
        first_carried = 7 + owners
        outs = pl.pallas_call(
            functools.partial(
                result_kernel, chunk=chunk, part=part, owners=owners, carried=carried
            ),
            out_shape=(jax.ShapeDtypeStruct((tokens, columns), BF16),) * 4,
            grid_spec=pltpu.PrefetchScalarGridSpec(
                num_scalar_prefetch=1,
                grid=(owners,),
                in_specs=[row_spec, col_spec]
                + [token_specs(chunk)] * 4
                + [state_spec] * owners
                + [pl.BlockSpec(memory_space=pl.ANY)] * carried,
                out_specs=(token_specs(chunk),) * 4,
                scratch_shapes=[pltpu.VMEM((2, part, width, width), BF16)],
            ),
            input_output_aliases={first_carried + i: i for i in range(carried)},
            cost_estimate=pl.CostEstimate(
                flops=12 * tokens * tokens * columns // chunks,
                bytes_accessed=16 * tokens * columns // chunks,
                transcendentals=0,
            ),
            compiler_params=params(),
            name=f"result{chunk}",
        )(place, rows, cols, *inputs, *states, *(outs or ()))
    return tuple(outs)


def solution(mesh):
    spec = P((SEQ, HEAD), None)
    body = functools.partial(on_device, seq_size=mesh.shape[SEQ], owners=mesh.shape[HEAD])
    return jax.shard_map(
        body,
        mesh=mesh,
        in_specs=(spec, spec, spec, spec, P(HEAD, SEQ)),
        out_specs=(spec, spec, spec, spec),
        check_vma=False,
    )
```

```python
import functools

import jax
import jax.numpy as jnp
from jax import lax
from jax.experimental import pallas as pl
from jax.experimental.pallas import tpu as pltpu
from jax.sharding import PartitionSpec as P


SEQ = "seq"
HEAD = "head"
PAIR = 2
F32 = jnp.float32
BF16 = jnp.bfloat16


def dot(a, b, contract, precision=None):
    return lax.dot_general(
        a, b, (((contract[0],), (contract[1],)), ((), ())),
        precision=precision, preferred_element_type=F32,
    )


def params(mib=16):
    return pltpu.CompilerParams(vmem_limit_bytes=mib << 20)


def split(x):
    high = x.astype(BF16)
    rest = x - high.astype(F32)
    middle = rest.astype(BF16)
    return high, middle, (rest - middle.astype(F32)).astype(BF16)


def prepare(decay_refs, row_ref, col_ref):
    me = lax.axis_index(HEAD)
    owners = len(decay_refs)
    heads, tokens = row_ref.shape[1:]
    at = lax.broadcasted_iota(jnp.int32, (tokens, tokens), 0)
    by = lax.broadcasted_iota(jnp.int32, (tokens, tokens), 1)
    upto = (at <= by).astype(BF16)
    since = (by <= at).astype(BF16)
    start = pl.multiple_of(me * tokens, tokens)
    own = jnp.concatenate([ref[:, pl.ds(start, tokens)] for ref in decay_refs], axis=0)
    pieces = split(own)
    rows = sum(dot(piece, upto, (1, 0)) for piece in pieces)
    cols = sum(dot(since, piece, (1, 1)) for piece in pieces)
    for slot in range(owners):
        row_ref[slot] = rows[slot * heads : (slot + 1) * heads]
        col_ref[slot] = cols[:, slot * heads : (slot + 1) * heads]


def summarize(row_ref, columns_of, out_refs, low, part):
    _, tokens = row_ref.shape[1:]
    width = out_refs[0].shape[-1]
    scale = width ** (-0.5)
    for slot, out_ref in enumerate(out_refs):
        owner = lax.axis_index(HEAD) ^ slot
        row = row_ref[slot]
        weight = jnp.exp(-(row[:, tokens - 1 : tokens] - row))
        growth = jnp.exp(-row)
        for member in range(part):
            head = low + member
            q, k, v, g = columns_of(slot, owner, member)
            keyed = (k.T.astype(F32) * weight[head : head + 1]).astype(BF16)
            queried = (q.T.astype(F32) * growth[head : head + 1]).astype(BF16)
            out_ref[0, member] = dot(keyed, v, (1, 0)).astype(BF16)
            out_ref[1, member] = (scale * dot(queried, g, (1, 0))).astype(BF16)


def first_kernel(_, *refs, part, owners):
    decay_refs, refs = refs[:owners], refs[owners:]
    token_refs, refs = refs[:4], refs[4:]
    row_ref, col_ref, *out_refs, held, sems = refs
    heads = row_ref.shape[1]
    width = out_refs[0].shape[-1]
    copies = []
    for slot in range(owners):
        owner = lax.axis_index(HEAD) ^ slot
        cols = pl.ds(pl.multiple_of(owner * heads * width, width), part * width)
        copies.append(
            [
                pltpu.make_async_copy(ref.at[:, cols], held.at[index, slot], sems.at[index, slot])
                for index, ref in enumerate(token_refs)
            ]
        )
        for copy in copies[-1]:
            copy.start()
    prepare(decay_refs, row_ref, col_ref)

    def columns_of(slot, owner, member):
        if member == 0:
            for copy in copies[slot]:
                copy.wait()
        cols = slice(member * width, (member + 1) * width)
        return [held[index, slot, :, cols] for index in range(4)]

    summarize(row_ref, columns_of, out_refs, 0, part)


def later_kernel(row_ref, *refs, low, part):
    token_refs, out_refs = refs[:4], refs[4:]
    heads = row_ref.shape[1]
    width = out_refs[0].shape[-1]

    def columns_of(slot, owner, member):
        start = (owner * heads + low + member) * width
        return [ref[:, pl.ds(pl.multiple_of(start, width), width)] for ref in token_refs]

    summarize(row_ref, columns_of, out_refs, low, part)


def link_layout(owners):
    sizes = dict(near0=owners * owners, near1=owners * owners, after=owners, before=owners, block=1)
    at, total = {}, 0
    for name, size in sizes.items():
        at[name] = total
        total += size
    return sizes, at, -(-total // 8) * 8


def link_kernel(decay_ref, w_ref, *, owners):
    me = lax.axis_index(HEAD)
    sizes, at, length = link_layout(owners)
    heads = decay_ref.shape[0]
    tokens = decay_ref.shape[1] // owners
    index = lax.broadcasted_iota(jnp.int32, (length, 1), 0)
    low = high = keep = jnp.zeros((length, 1), jnp.int32)

    def put(name, low_, high_, keep_):
        nonlocal low, high, keep
        here = (index >= at[name]) & (index < at[name] + sizes[name])
        low = jnp.where(here, low_, low)
        high = jnp.where(here, high_, high)
        keep = jnp.where(here, jnp.where(keep_, 1, 0), keep)

    for side in range(2):
        r = index - at[f"near{side}"]
        to = me ^ lax.div(r, owners)
        of = me ^ lax.rem(r, owners)
        if side == 0:
            put("near0", of, to, of < to)
        else:
            put("near1", to, of, to < of)
    put("after", me ^ (index - at["after"]), owners, index >= 0)
    put("before", -1, me ^ (index - at["before"]), index >= 0)
    put("block", -1, owners, index >= 0)
    spot = lax.broadcasted_iota(jnp.int32, (length, owners * tokens), 1)
    inside = ((spot >= (low + 1) * tokens) & (spot < high * tokens)).astype(BF16)
    total = sum(dot(inside, piece, (1, 1)) for piece in split(decay_ref[...]))
    weight = jnp.where(keep > 0, jnp.exp(-total), 0.0)
    weight = jnp.where(index == at["block"], total, weight)
    for head in range(heads):
        w_ref[head] = jnp.broadcast_to(weight[:, head : head + 1], w_ref.shape[1:])


def extra_rows(part):
    return -(-3 * part // 16) * 16


def log_rows(logs):
    part, lanes = logs.shape
    rows = [piece.astype(F32) for piece in split(logs)]
    rows.append(jnp.zeros((extra_rows(part) - 3 * part, lanes), F32))
    return jnp.concatenate(rows, axis=0).astype(BF16)


def get_logs(ref, part):
    rows = ref[ref.shape[0] - extra_rows(part) :].astype(F32)
    return rows[:part] + rows[part : 2 * part] + rows[2 * part : 3 * part]


def total_kernel(w_ref, *refs, low, part, at, owners):
    out_ref = refs[-1]
    width = out_ref.shape[1]
    for side, name in enumerate(("after", "before")):
        for member in range(part):
            total = 0.0
            for slot, ref in enumerate(refs[:owners]):
                index = at[name] + slot
                total = total + w_ref[low + member, index : index + 1] * ref[side, member].astype(F32)
            rows = slice((side * part + member) * width, (side * part + member + 1) * width)
            out_ref[rows] = total.astype(BF16)
    index = at["block"]
    logs = jnp.concatenate([w_ref[low + m, index : index + 1] for m in range(part)], axis=0)
    out_ref[2 * part * width :] = log_rows(logs)


def pair_kernel(own_ref, other_ref, *out_refs, part):
    far_at = lax.div(lax.axis_index(SEQ), PAIR)
    lead = lax.rem(lax.axis_index(SEQ), PAIR) == 0
    width = own_ref.shape[1]
    own_logs, other_logs = get_logs(own_ref, part), get_logs(other_ref, part)
    over_own, over_other = jnp.exp(-own_logs), jnp.exp(-other_logs)
    weights = (
        (jnp.where(lead, over_other, 1.0), jnp.where(lead, 1.0, over_own)),
        (jnp.where(lead, 1.0, over_other), jnp.where(lead, over_own, 1.0)),
    )
    both_logs = log_rows(own_logs + other_logs)
    for member in range(part):
        both = []
        for side, (own, other) in enumerate(weights):
            rows = slice((side * part + member) * width, (side * part + member + 1) * width)
            both.append(
                own[member : member + 1] * own_ref[rows].astype(F32)
                + other[member : member + 1] * other_ref[rows].astype(F32)
            )
        both = [value.astype(BF16) for value in both]
        for slot, out_ref in enumerate(out_refs):
            onward = (far_at ^ (slot + 1)) > far_at
            rows = slice(member * width, (member + 1) * width)
            out_ref[rows] = jnp.where(onward, both[0], both[1])
    for out_ref in out_refs:
        out_ref[part * width :] = both_logs


def state_kernel(w_ref, *refs, low, part, at, owners, far):
    far_at = lax.div(lax.axis_index(SEQ), PAIR)
    lead = lax.rem(lax.axis_index(SEQ), PAIR) == 0
    ins = refs[:owners]
    other_ref = refs[owners]
    far_refs = refs[owners + 1 : owners + 1 + far]
    out_refs = refs[owners + 1 + far :]
    width = other_ref.shape[1]
    other_logs = get_logs(other_ref, part)
    far_logs = [get_logs(ref, part) for ref in far_refs]
    sources = [far_at ^ (slot + 1) for slot in range(far)]
    for side, enter in enumerate(("before", "after")):
        here = lead if side == 1 else jnp.logical_not(lead)
        gone = jnp.where(here, other_logs, 0.0)
        factors = []
        for source in sources:
            use = source < far_at if side == 0 else source > far_at
            log = gone
            for between, logs in zip(sources, far_logs):
                if side == 0:
                    inside = (between > source) & (between < far_at)
                else:
                    inside = (between < source) & (between > far_at)
                log = log + jnp.where(inside, logs, 0.0)
            factors.append(jnp.where(use, jnp.exp(-log), 0.0))
        for member in range(part):
            rows = slice((side * part + member) * width, (side * part + member + 1) * width)
            base = jnp.where(here, other_ref[rows].astype(F32), 0.0)
            rows = slice(member * width, (member + 1) * width)
            for factor, ref in zip(factors, far_refs):
                base = base + factor[member : member + 1] * ref[rows].astype(F32)
            pieces = [ref[side, member].astype(F32) for ref in ins]
            for slot, out_ref in enumerate(out_refs):
                index = at[enter] + slot
                value = w_ref[low + member, index : index + 1] * base
                for source, piece in enumerate(pieces):
                    if source != slot:
                        index = at[f"near{side}"] + slot * owners + source
                        value = value + w_ref[low + member, index : index + 1] * piece
                out_ref[side, member] = value.astype(BF16)


def inner_parts(row, col, q, k, v, g):
    tokens, width = q.shape
    scale = width ** (-0.5)
    at = lax.broadcasted_iota(jnp.int32, (tokens, tokens), 0)
    by = lax.broadcasted_iota(jnp.int32, (tokens, tokens), 1)
    causal = at >= by
    mask = jnp.where(causal, scale * jnp.exp(-jnp.where(causal, col - row, 0.0)), 0.0)
    scores = (dot(q, k, (1, 1)) * mask).astype(BF16)
    grads = (dot(g, v, (1, 1)) * mask).astype(BF16)
    return (
        dot(scores, v, (1, 0)),
        dot(grads, k, (1, 0)),
        dot(grads, q, (0, 0)),
        dot(scores, g, (0, 0)),
    )


def inner_kernel(row_ref, col_ref, q_ref, k_ref, v_ref, g_ref, *refs, low, part, owners):
    part_refs, scaled_refs = refs[:4], refs[4:]
    heads, tokens = row_ref.shape[1:]
    width = part_refs[0].shape[2] // part
    scale = width ** (-0.5)
    for slot in range(owners):
        owner = lax.axis_index(HEAD) ^ slot
        for member in range(part):
            head = low + member
            cols = pl.ds(pl.multiple_of((owner * heads + head) * width, width), width)
            here = slice(member * width, (member + 1) * width)
            row = row_ref[slot][head : head + 1, :]
            col = col_ref[slot][:, head : head + 1]
            weight = jnp.exp(-(row[:, tokens - 1 : tokens] - col))
            growth = scale * jnp.exp(-col)
            q, k, v, g = q_ref[:, cols], k_ref[:, cols], v_ref[:, cols], g_ref[:, cols]
            for ref, value in zip(part_refs, inner_parts(row, col, q, k, v, g)):
                ref[slot, :, here] = value
            for ref, rows, factor in zip(scaled_refs, (q, g, v, k), (growth, growth, weight, weight)):
                ref[slot, :, here] = (rows.astype(F32) * factor).astype(BF16)


def result_kernel(*refs, low, part, owners, slots, carried):
    state_refs, refs = refs[: len(slots)], refs[len(slots) :]
    part_refs, scaled_refs, refs = refs[:4], refs[4:8], refs[8 + carried :]
    out_refs, held, sems = refs[:4], *refs[4:]
    width = held.shape[3] // part
    heads = out_refs[0].shape[1] // (owners * width)
    copies = []
    for slot, state_ref in zip(slots, state_refs):
        for member in range(part):
            here = slice(member * width, (member + 1) * width)
            for index in range(4):
                state = state_ref[index // 2, member]
                turned = index in (1, 2)
                value = dot(scaled_refs[index][slot, :, here], state, (1, 1 if turned else 0))
                held[index, slot, :, here] = (part_refs[index][slot, :, here] + value).astype(BF16)
        start = ((lax.axis_index(HEAD) ^ slot) * heads + low) * width
        cols = pl.ds(pl.multiple_of(start, width), part * width)
        for index, out_ref in enumerate(out_refs):
            copy = pltpu.make_async_copy(
                held.at[index, slot], out_ref.at[:, cols], sems.at[index, slot]
            )
            copy.start()
            copies.append(copy)
    for copy in copies:
        copy.wait()


def chunk_sizes(heads):
    return [heads - heads // 2, heads // 2] if heads >= 2 else [heads]


def on_device(query_rows, key_rows, value_rows, out_grad, decay, *, seq_size, owners):
    heads = decay.shape[0]
    tokens, columns = query_rows.shape
    width = columns // (heads * owners)
    chunks = chunk_sizes(heads)
    chunks = [(sum(chunks[:i]), part) for i, part in enumerate(chunks)]
    far = seq_size // PAIR - 1
    _, at, table = link_layout(owners)

    def swap(array, axis, size, offset):
        return lax.ppermute(array, axis, [(i, i ^ offset) for i in range(size)])

    def exchange(arrays):
        return [arrays[0]] + [swap(arrays[slot], HEAD, owners, slot) for slot in range(1, owners)]

    whole = pl.BlockSpec(memory_space=pltpu.VMEM)
    row_shape = jax.ShapeDtypeStruct((owners, heads, tokens), F32)
    col_shape = jax.ShapeDtypeStruct((owners, tokens, heads), F32)
    inputs = (query_rows, key_rows, value_rows, out_grad)

    def state_shapes(part):
        return (jax.ShapeDtypeStruct((2, part, width, width), BF16),) * owners

    def cost(flops, passes, part):
        share = tokens * owners * part * width
        return pl.CostEstimate(flops=flops * share, bytes_accessed=2 * passes * share, transcendentals=0)

    decays = exchange([decay] * owners)
    hbm = pl.BlockSpec(memory_space=pltpu.HBM)
    anywhere = pl.BlockSpec(memory_space=pl.ANY)
    weights = pl.pallas_call(
        functools.partial(link_kernel, owners=owners),
        out_shape=jax.ShapeDtypeStruct((heads, table, width), F32),
        in_specs=[whole],
        out_specs=whole,
        cost_estimate=pl.CostEstimate(flops=0, bytes_accessed=24 * tokens * columns, transcendentals=0),
        compiler_params=params(),
        name="link",
    )(decay)
    part = chunks[0][1]
    rows, cols, *first = pl.pallas_call(
        functools.partial(first_kernel, part=part, owners=owners),
        out_shape=(row_shape, col_shape) + state_shapes(part),
        in_specs=[anywhere] + [whole] * owners + [hbm] * 4,
        out_specs=(whole,) * (2 + owners),
        scratch_shapes=[
            pltpu.VMEM((4, owners, tokens, part * width), BF16),
            pltpu.SemaphoreType.DMA((4, owners)),
        ],
        cost_estimate=cost(4 * width, 4, part),
        compiler_params=params(),
        name="first",
    )(weights, *decays, *[pltpu.with_memory_space_constraint(x, pltpu.HBM) for x in inputs])
    summaries = [first]
    for low, part in chunks[1:]:
        summary_call = pl.pallas_call(
            functools.partial(later_kernel, low=low, part=part),
            out_shape=state_shapes(part),
            in_specs=[whole] * 5,
            out_specs=(whole,) * owners,
            cost_estimate=cost(4 * width, 4, part),
            compiler_params=params(),
        )
        summaries.append(summary_call(rows, *inputs))

    outs = None
    for chunk, (low, part) in enumerate(chunks):
        total_shape = jax.ShapeDtypeStruct((2 * part * width + extra_rows(part), width), BF16)
        far_shape = jax.ShapeDtypeStruct((part * width + extra_rows(part), width), BF16)
        part_shape = jax.ShapeDtypeStruct((owners, tokens, part * width), F32)
        scaled_shape = jax.ShapeDtypeStruct((owners, tokens, part * width), BF16)
        own = summaries[chunk]
        here = exchange(own)
        total_call = pl.pallas_call(
            functools.partial(total_kernel, low=low, part=part, at=at, owners=owners),
            out_shape=total_shape,
            in_specs=[whole] * (owners + 1),
            out_specs=whole,
            compiler_params=params(),
        )
        total = total_call(weights, *here)
        other = swap(total, SEQ, seq_size, 1)
        sent = pl.pallas_call(
            functools.partial(pair_kernel, part=part),
            out_shape=(far_shape,) * far,
            in_specs=[whole, whole],
            out_specs=(whole,) * far,
            compiler_params=params(),
        )(total, other)
        heard = [swap(array, SEQ, seq_size, PAIR * (slot + 1)) for slot, array in enumerate(sent)]
        state_call = pl.pallas_call(
            functools.partial(
                state_kernel, low=low, part=part, at=at, owners=owners, far=far
            ),
            out_shape=state_shapes(part),
            in_specs=[whole] * (owners + far + 2),
            out_specs=(whole,) * owners,
            compiler_params=params(),
        )
        states = state_call(weights, *here, other, *heard)
        states = exchange(states)
        inner_call = pl.pallas_call(
            functools.partial(inner_kernel, low=low, part=part, owners=owners),
            out_shape=(part_shape,) * 4 + (scaled_shape,) * 4,
            in_specs=[whole] * 6,
            out_specs=(whole,) * 8,
            cost_estimate=cost(12 * tokens, 12, part),
            compiler_params=params(),
        )
        parts = inner_call(rows, cols, *inputs)
        for slots in (range(1), range(1, owners)) if chunk == len(chunks) - 1 else (range(owners),):
            carried = 0 if outs is None else 4
            first_carried = 8 + len(slots)
            outs = pl.pallas_call(
                functools.partial(
                    result_kernel,
                    low=low,
                    part=part,
                    owners=owners,
                    slots=tuple(slots),
                    carried=carried,
                ),
                out_shape=(jax.ShapeDtypeStruct((tokens, columns), BF16),) * 4,
                in_specs=[whole] * (8 + len(slots)) + [hbm] * carried,
                out_specs=(hbm,) * 4,
                scratch_shapes=[
                    pltpu.VMEM((4, owners, tokens, part * width), BF16),
                    pltpu.SemaphoreType.DMA((4, owners)),
                ],
                input_output_aliases={first_carried + i: i for i in range(carried)},
                cost_estimate=cost(8 * width, 8, part),
                compiler_params=params(),
            )(*[states[slot] for slot in slots], *parts, *(outs or ()))
    return tuple(outs)


def solution(mesh):
    spec = P((SEQ, HEAD), None)

    def body(*args):
        return on_device(*args, seq_size=mesh.shape[SEQ], owners=mesh.shape[HEAD])

    return jax.shard_map(
        body,
        mesh=mesh,
        in_specs=(spec, spec, spec, spec, P(HEAD, SEQ)),
        out_specs=(spec, spec, spec, spec),
        check_vma=False,
    )
```

```python
import functools

import jax
import jax.numpy as jnp
from jax import lax
from jax.experimental import pallas as pl
from jax.experimental.pallas import tpu as pltpu
from jax.sharding import PartitionSpec as P


SEQ = "seq"
HEAD = "head"
PAIR = 2
F32 = jnp.float32
BF16 = jnp.bfloat16


def dot(a, b, contract, precision=None):
    return lax.dot_general(
        a, b, (((contract[0],), (contract[1],)), ((), ())),
        precision=precision, preferred_element_type=F32,
    )


def params(mib=16):
    return pltpu.CompilerParams(vmem_limit_bytes=mib << 20)


def split(x):
    high = x.astype(BF16)
    rest = x - high.astype(F32)
    middle = rest.astype(BF16)
    return high, middle, (rest - middle.astype(F32)).astype(BF16)


def prepare(decay_refs, row_ref, col_ref):
    me = lax.axis_index(HEAD)
    owners = len(decay_refs)
    heads, tokens = row_ref.shape[1:]
    at = lax.broadcasted_iota(jnp.int32, (tokens, tokens), 0)
    by = lax.broadcasted_iota(jnp.int32, (tokens, tokens), 1)
    upto = (at <= by).astype(BF16)
    since = (by <= at).astype(BF16)
    start = pl.multiple_of(me * tokens, tokens)
    own = jnp.concatenate([ref[:, pl.ds(start, tokens)] for ref in decay_refs], axis=0)
    pieces = split(own)
    rows = sum(dot(piece, upto, (1, 0)) for piece in pieces)
    cols = sum(dot(since, piece, (1, 1)) for piece in pieces)
    for slot in range(owners):
        row_ref[slot] = rows[slot * heads : (slot + 1) * heads]
        col_ref[slot] = cols[:, slot * heads : (slot + 1) * heads]


def summarize(row_ref, columns_of, out_refs, low, part):
    _, tokens = row_ref.shape[1:]
    width = out_refs[0].shape[-1]
    scale = width ** (-0.5)
    for slot, out_ref in enumerate(out_refs):
        owner = lax.axis_index(HEAD) ^ slot
        row = row_ref[slot]
        weight = jnp.exp(-(row[:, tokens - 1 : tokens] - row))
        growth = jnp.exp(-row)
        for member in range(part):
            head = low + member
            q, k, v, g = columns_of(slot, owner, member)
            keyed = (k.T.astype(F32) * weight[head : head + 1]).astype(BF16)
            queried = (q.T.astype(F32) * growth[head : head + 1]).astype(BF16)
            out_ref[0, member] = dot(keyed, v, (1, 0)).astype(BF16)
            out_ref[1, member] = (scale * dot(queried, g, (1, 0))).astype(BF16)


def first_kernel(_, *refs, part, owners):
    decay_refs, refs = refs[:owners], refs[owners:]
    token_refs, refs = refs[:4], refs[4:]
    row_ref, col_ref, *out_refs, held, sems = refs
    heads = row_ref.shape[1]
    width = out_refs[0].shape[-1]
    copies = []
    for slot in range(owners):
        owner = lax.axis_index(HEAD) ^ slot
        cols = pl.ds(pl.multiple_of(owner * heads * width, width), part * width)
        copies.append(
            [
                pltpu.make_async_copy(ref.at[:, cols], held.at[index, slot], sems.at[index, slot])
                for index, ref in enumerate(token_refs)
            ]
        )
        for copy in copies[-1]:
            copy.start()
    prepare(decay_refs, row_ref, col_ref)

    def columns_of(slot, owner, member):
        if member == 0:
            for copy in copies[slot]:
                copy.wait()
        cols = slice(member * width, (member + 1) * width)
        return [held[index, slot, :, cols] for index in range(4)]

    summarize(row_ref, columns_of, out_refs, 0, part)


def later_kernel(row_ref, *refs, low, part):
    token_refs, out_refs = refs[:4], refs[4:]
    heads = row_ref.shape[1]
    width = out_refs[0].shape[-1]

    def columns_of(slot, owner, member):
        start = (owner * heads + low + member) * width
        return [ref[:, pl.ds(pl.multiple_of(start, width), width)] for ref in token_refs]

    summarize(row_ref, columns_of, out_refs, low, part)


def link_layout(owners):
    sizes = dict(near0=owners * owners, near1=owners * owners, after=owners, before=owners, block=1)
    at, total = {}, 0
    for name, size in sizes.items():
        at[name] = total
        total += size
    return sizes, at, -(-total // 8) * 8


def link_kernel(decay_ref, w_ref, *, owners):
    me = lax.axis_index(HEAD)
    sizes, at, length = link_layout(owners)
    heads = decay_ref.shape[0]
    tokens = decay_ref.shape[1] // owners
    index = lax.broadcasted_iota(jnp.int32, (length, 1), 0)
    low = high = keep = jnp.zeros((length, 1), jnp.int32)

    def put(name, low_, high_, keep_):
        nonlocal low, high, keep
        here = (index >= at[name]) & (index < at[name] + sizes[name])
        low = jnp.where(here, low_, low)
        high = jnp.where(here, high_, high)
        keep = jnp.where(here, jnp.where(keep_, 1, 0), keep)

    for side in range(2):
        r = index - at[f"near{side}"]
        to = me ^ lax.div(r, owners)
        of = me ^ lax.rem(r, owners)
        if side == 0:
            put("near0", of, to, of < to)
        else:
            put("near1", to, of, to < of)
    put("after", me ^ (index - at["after"]), owners, index >= 0)
    put("before", -1, me ^ (index - at["before"]), index >= 0)
    put("block", -1, owners, index >= 0)
    spot = lax.broadcasted_iota(jnp.int32, (length, owners * tokens), 1)
    inside = ((spot >= (low + 1) * tokens) & (spot < high * tokens)).astype(BF16)
    total = sum(dot(inside, piece, (1, 1)) for piece in split(decay_ref[...]))
    weight = jnp.where(keep > 0, jnp.exp(-total), 0.0)
    weight = jnp.where(index == at["block"], total, weight)
    for head in range(heads):
        w_ref[head] = jnp.broadcast_to(weight[:, head : head + 1], w_ref.shape[1:])


def extra_rows(part):
    return -(-3 * part // 16) * 16


def log_rows(logs):
    part, lanes = logs.shape
    rows = [piece.astype(F32) for piece in split(logs)]
    rows.append(jnp.zeros((extra_rows(part) - 3 * part, lanes), F32))
    return jnp.concatenate(rows, axis=0).astype(BF16)


def get_logs(ref, part):
    rows = ref[ref.shape[0] - extra_rows(part) :].astype(F32)
    return rows[:part] + rows[part : 2 * part] + rows[2 * part : 3 * part]


def total_kernel(w_ref, *refs, low, part, at, owners):
    out_ref = refs[-1]
    width = out_ref.shape[1]
    for side, name in enumerate(("after", "before")):
        for member in range(part):
            total = 0.0
            for slot, ref in enumerate(refs[:owners]):
                index = at[name] + slot
                total = total + w_ref[low + member, index : index + 1] * ref[side, member].astype(F32)
            rows = slice((side * part + member) * width, (side * part + member + 1) * width)
            out_ref[rows] = total.astype(BF16)
    index = at["block"]
    logs = jnp.concatenate([w_ref[low + m, index : index + 1] for m in range(part)], axis=0)
    out_ref[2 * part * width :] = log_rows(logs)


def pair_kernel(own_ref, other_ref, *out_refs, part):
    far_at = lax.div(lax.axis_index(SEQ), PAIR)
    lead = lax.rem(lax.axis_index(SEQ), PAIR) == 0
    width = own_ref.shape[1]
    own_logs, other_logs = get_logs(own_ref, part), get_logs(other_ref, part)
    over_own, over_other = jnp.exp(-own_logs), jnp.exp(-other_logs)
    weights = (
        (jnp.where(lead, over_other, 1.0), jnp.where(lead, 1.0, over_own)),
        (jnp.where(lead, 1.0, over_other), jnp.where(lead, over_own, 1.0)),
    )
    both_logs = log_rows(own_logs + other_logs)
    for member in range(part):
        both = []
        for side, (own, other) in enumerate(weights):
            rows = slice((side * part + member) * width, (side * part + member + 1) * width)
            both.append(
                own[member : member + 1] * own_ref[rows].astype(F32)
                + other[member : member + 1] * other_ref[rows].astype(F32)
            )
        both = [value.astype(BF16) for value in both]
        for slot, out_ref in enumerate(out_refs):
            onward = (far_at ^ (slot + 1)) > far_at
            rows = slice(member * width, (member + 1) * width)
            out_ref[rows] = jnp.where(onward, both[0], both[1])
    for out_ref in out_refs:
        out_ref[part * width :] = both_logs


def state_kernel(w_ref, *refs, low, part, at, owners, far):
    far_at = lax.div(lax.axis_index(SEQ), PAIR)
    lead = lax.rem(lax.axis_index(SEQ), PAIR) == 0
    ins = refs[:owners]
    other_ref = refs[owners]
    far_refs = refs[owners + 1 : owners + 1 + far]
    out_refs = refs[owners + 1 + far :]
    width = other_ref.shape[1]
    other_logs = get_logs(other_ref, part)
    far_logs = [get_logs(ref, part) for ref in far_refs]
    sources = [far_at ^ (slot + 1) for slot in range(far)]
    for side, enter in enumerate(("before", "after")):
        here = lead if side == 1 else jnp.logical_not(lead)
        gone = jnp.where(here, other_logs, 0.0)
        factors = []
        for source in sources:
            use = source < far_at if side == 0 else source > far_at
            log = gone
            for between, logs in zip(sources, far_logs):
                if side == 0:
                    inside = (between > source) & (between < far_at)
                else:
                    inside = (between < source) & (between > far_at)
                log = log + jnp.where(inside, logs, 0.0)
            factors.append(jnp.where(use, jnp.exp(-log), 0.0))
        for member in range(part):
            rows = slice((side * part + member) * width, (side * part + member + 1) * width)
            base = jnp.where(here, other_ref[rows].astype(F32), 0.0)
            rows = slice(member * width, (member + 1) * width)
            for factor, ref in zip(factors, far_refs):
                base = base + factor[member : member + 1] * ref[rows].astype(F32)
            pieces = [ref[side, member].astype(F32) for ref in ins]
            for slot, out_ref in enumerate(out_refs):
                index = at[enter] + slot
                value = w_ref[low + member, index : index + 1] * base
                for source, piece in enumerate(pieces):
                    if source != slot:
                        index = at[f"near{side}"] + slot * owners + source
                        value = value + w_ref[low + member, index : index + 1] * piece
                out_ref[side, member] = value.astype(BF16)


def inner_parts(row, col, q, k, v, g):
    tokens, width = q.shape
    scale = width ** (-0.5)
    at = lax.broadcasted_iota(jnp.int32, (tokens, tokens), 0)
    by = lax.broadcasted_iota(jnp.int32, (tokens, tokens), 1)
    causal = at >= by
    mask = jnp.where(causal, scale * jnp.exp(-jnp.where(causal, col - row, 0.0)), 0.0)
    scores = (dot(q, k, (1, 1)) * mask).astype(BF16)
    grads = (dot(g, v, (1, 1)) * mask).astype(BF16)
    return (
        dot(scores, v, (1, 0)),
        dot(grads, k, (1, 0)),
        dot(grads, q, (0, 0)),
        dot(scores, g, (0, 0)),
    )


def inner_kernel(row_ref, col_ref, q_ref, k_ref, v_ref, g_ref, *refs, low, part, owners):
    part_refs, scaled_refs = refs[:4], refs[4:]
    heads, tokens = row_ref.shape[1:]
    width = part_refs[0].shape[2] // part
    scale = width ** (-0.5)
    for slot in range(owners):
        owner = lax.axis_index(HEAD) ^ slot
        for member in range(part):
            head = low + member
            cols = pl.ds(pl.multiple_of((owner * heads + head) * width, width), width)
            here = slice(member * width, (member + 1) * width)
            row = row_ref[slot][head : head + 1, :]
            col = col_ref[slot][:, head : head + 1]
            weight = jnp.exp(-(row[:, tokens - 1 : tokens] - col))
            growth = scale * jnp.exp(-col)
            q, k, v, g = q_ref[:, cols], k_ref[:, cols], v_ref[:, cols], g_ref[:, cols]
            for ref, value in zip(part_refs, inner_parts(row, col, q, k, v, g)):
                ref[slot, :, here] = value
            for ref, rows, factor in zip(scaled_refs, (q, g, v, k), (growth, growth, weight, weight)):
                ref[slot, :, here] = (rows.astype(F32) * factor).astype(BF16)


def result_kernel(*refs, low, part, owners, slots, carried):
    state_refs, refs = refs[: len(slots)], refs[len(slots) :]
    part_refs, scaled_refs, refs = refs[:4], refs[4:8], refs[8 + carried :]
    out_refs, held, sems = refs[:4], *refs[4:]
    width = held.shape[3] // part
    heads = out_refs[0].shape[1] // (owners * width)
    copies = []
    for slot, state_ref in zip(slots, state_refs):
        for member in range(part):
            here = slice(member * width, (member + 1) * width)
            for index in range(4):
                state = state_ref[index // 2, member]
                turned = index in (1, 2)
                value = dot(scaled_refs[index][slot, :, here], state, (1, 1 if turned else 0))
                held[index, slot, :, here] = (part_refs[index][slot, :, here] + value).astype(BF16)
        start = ((lax.axis_index(HEAD) ^ slot) * heads + low) * width
        cols = pl.ds(pl.multiple_of(start, width), part * width)
        for index, out_ref in enumerate(out_refs):
            copy = pltpu.make_async_copy(
                held.at[index, slot], out_ref.at[:, cols], sems.at[index, slot]
            )
            copy.start()
            copies.append(copy)
    for copy in copies:
        copy.wait()


def chunk_sizes(heads):
    return [heads - heads // 2, heads // 2] if heads >= 2 else [heads]


def on_device(query_rows, key_rows, value_rows, out_grad, decay, *, seq_size, owners):
    heads = decay.shape[0]
    tokens, columns = query_rows.shape
    width = columns // (heads * owners)
    chunks = chunk_sizes(heads)
    chunks = [(sum(chunks[:i]), part) for i, part in enumerate(chunks)]
    far = seq_size // PAIR - 1
    _, at, table = link_layout(owners)

    def swap(array, axis, size, offset):
        return lax.ppermute(array, axis, [(i, i ^ offset) for i in range(size)])

    def exchange(arrays):
        return [arrays[0]] + [swap(arrays[slot], HEAD, owners, slot) for slot in range(1, owners)]

    whole = pl.BlockSpec(memory_space=pltpu.VMEM)
    row_shape = jax.ShapeDtypeStruct((owners, heads, tokens), F32)
    col_shape = jax.ShapeDtypeStruct((owners, tokens, heads), F32)
    inputs = (query_rows, key_rows, value_rows, out_grad)

    def state_shapes(part):
        return (jax.ShapeDtypeStruct((2, part, width, width), BF16),) * owners

    def cost(flops, passes, part):
        share = tokens * owners * part * width
        return pl.CostEstimate(flops=flops * share, bytes_accessed=2 * passes * share, transcendentals=0)

    decays = exchange([decay] * owners)
    hbm = pl.BlockSpec(memory_space=pltpu.HBM)
    anywhere = pl.BlockSpec(memory_space=pl.ANY)
    weights = pl.pallas_call(
        functools.partial(link_kernel, owners=owners),
        out_shape=jax.ShapeDtypeStruct((heads, table, width), F32),
        in_specs=[whole],
        out_specs=whole,
        cost_estimate=pl.CostEstimate(flops=0, bytes_accessed=24 * tokens * columns, transcendentals=0),
        compiler_params=params(),
        name="link",
    )(decay)
    part = chunks[0][1]
    rows, cols, *first = pl.pallas_call(
        functools.partial(first_kernel, part=part, owners=owners),
        out_shape=(row_shape, col_shape) + state_shapes(part),
        in_specs=[anywhere] + [whole] * owners + [hbm] * 4,
        out_specs=(whole,) * (2 + owners),
        scratch_shapes=[
            pltpu.VMEM((4, owners, tokens, part * width), BF16),
            pltpu.SemaphoreType.DMA((4, owners)),
        ],
        cost_estimate=cost(4 * width, 4, part),
        compiler_params=params(),
        name="first",
    )(weights, *decays, *[pltpu.with_memory_space_constraint(x, pltpu.HBM) for x in inputs])
    summaries = [first]
    for low, part in chunks[1:]:
        summary_call = pl.pallas_call(
            functools.partial(later_kernel, low=low, part=part),
            out_shape=state_shapes(part),
            in_specs=[whole] * 5,
            out_specs=(whole,) * owners,
            cost_estimate=cost(4 * width, 4, part),
            compiler_params=params(),
        )
        summaries.append(summary_call(rows, *inputs))

    outs = None
    for chunk, (low, part) in enumerate(chunks):
        total_shape = jax.ShapeDtypeStruct((2 * part * width + extra_rows(part), width), BF16)
        far_shape = jax.ShapeDtypeStruct((part * width + extra_rows(part), width), BF16)
        part_shape = jax.ShapeDtypeStruct((owners, tokens, part * width), F32)
        scaled_shape = jax.ShapeDtypeStruct((owners, tokens, part * width), BF16)
        own = summaries[chunk]
        here = exchange(own)
        total_call = pl.pallas_call(
            functools.partial(total_kernel, low=low, part=part, at=at, owners=owners),
            out_shape=total_shape,
            in_specs=[whole] * (owners + 1),
            out_specs=whole,
            compiler_params=params(),
        )
        total = total_call(weights, *here)
        other = swap(total, SEQ, seq_size, 1)
        pair_call = pl.pallas_call(
            functools.partial(pair_kernel, part=part),
            out_shape=(far_shape,) * far,
            in_specs=[whole, whole],
            out_specs=(whole,) * far,
            compiler_params=params(),
        )
        sent = pair_call(total, other)
        heard = [swap(array, SEQ, seq_size, PAIR * (slot + 1)) for slot, array in enumerate(sent)]
        state_call = pl.pallas_call(
            functools.partial(
                state_kernel, low=low, part=part, at=at, owners=owners, far=far
            ),
            out_shape=state_shapes(part),
            in_specs=[whole] * (owners + far + 2),
            out_specs=(whole,) * owners,
            compiler_params=params(),
        )
        states = state_call(weights, *here, other, *heard)
        states = exchange(states)
        inner_call = pl.pallas_call(
            functools.partial(inner_kernel, low=low, part=part, owners=owners),
            out_shape=(part_shape,) * 4 + (scaled_shape,) * 4,
            in_specs=[whole] * 6,
            out_specs=(whole,) * 8,
            cost_estimate=cost(12 * tokens, 12, part),
            compiler_params=params(),
        )
        parts = inner_call(rows, cols, *inputs)
        groups = [range(owners)]
        if chunk == len(chunks) - 1:
            half = owners // 2
            groups = [(0,), (half,), [slot for slot in range(1, owners) if slot != half]]
        for slots in groups:
            carried = 0 if outs is None else 4
            first_carried = 8 + len(slots)
            outs = pl.pallas_call(
                functools.partial(
                    result_kernel,
                    low=low,
                    part=part,
                    owners=owners,
                    slots=tuple(slots),
                    carried=carried,
                ),
                out_shape=(jax.ShapeDtypeStruct((tokens, columns), BF16),) * 4,
                in_specs=[whole] * (8 + len(slots)) + [hbm] * carried,
                out_specs=(hbm,) * 4,
                scratch_shapes=[
                    pltpu.VMEM((4, owners, tokens, part * width), BF16),
                    pltpu.SemaphoreType.DMA((4, owners)),
                ],
                input_output_aliases={first_carried + i: i for i in range(carried)},
                cost_estimate=cost(8 * width, 8, part),
                compiler_params=params(),
            )(*[states[slot] for slot in slots], *parts, *(outs or ()))
    return tuple(outs)


def solution(mesh):
    spec = P((SEQ, HEAD), None)

    def body(*args):
        return on_device(*args, seq_size=mesh.shape[SEQ], owners=mesh.shape[HEAD])

    return jax.shard_map(
        body,
        mesh=mesh,
        in_specs=(spec, spec, spec, spec, P(HEAD, SEQ)),
        out_specs=(spec, spec, spec, spec),
        check_vma=False,
    )
```

```python
import functools

import jax
import jax.numpy as jnp
from jax import lax
from jax.experimental import pallas as pl
from jax.experimental.pallas import tpu as pltpu
from jax.sharding import PartitionSpec as P


SEQ = "seq"
HEAD = "head"
PAIR = 2
F32 = jnp.float32
BF16 = jnp.bfloat16


def dot(a, b, contract, precision=None):
    return lax.dot_general(
        a, b, (((contract[0],), (contract[1],)), ((), ())),
        precision=precision, preferred_element_type=F32,
    )


def params(mib=16):
    return pltpu.CompilerParams(vmem_limit_bytes=mib << 20)


def split(x):
    high = x.astype(BF16)
    rest = x - high.astype(F32)
    middle = rest.astype(BF16)
    return high, middle, (rest - middle.astype(F32)).astype(BF16)


def prepare(decay_refs, row_ref, col_ref):
    me = lax.axis_index(HEAD)
    owners = len(decay_refs)
    heads, tokens = row_ref.shape[1:]
    at = lax.broadcasted_iota(jnp.int32, (tokens, tokens), 0)
    by = lax.broadcasted_iota(jnp.int32, (tokens, tokens), 1)
    upto = (at <= by).astype(BF16)
    since = (by <= at).astype(BF16)
    start = pl.multiple_of(me * tokens, tokens)
    own = jnp.concatenate([ref[:, pl.ds(start, tokens)] for ref in decay_refs], axis=0)
    pieces = split(own)
    rows = sum(dot(piece, upto, (1, 0)) for piece in pieces)
    cols = sum(dot(since, piece, (1, 1)) for piece in pieces)
    for slot in range(owners):
        row_ref[slot] = rows[slot * heads : (slot + 1) * heads]
        col_ref[slot] = cols[:, slot * heads : (slot + 1) * heads]


def summarize(row_ref, columns_of, out_refs, low, part):
    _, tokens = row_ref.shape[1:]
    width = out_refs[0].shape[-1]
    scale = width ** (-0.5)
    for slot, out_ref in enumerate(out_refs):
        row = row_ref[slot]
        weight = jnp.exp(-(row[:, tokens - 1 : tokens] - row))
        growth = jnp.exp(-row)
        for member in range(part):
            head = low + member
            q, k, v, g = columns_of(slot, member)
            keyed = (k.T.astype(F32) * weight[head : head + 1]).astype(BF16)
            queried = (q.T.astype(F32) * growth[head : head + 1]).astype(BF16)
            out_ref[0, member] = dot(keyed, v, (1, 0)).astype(BF16)
            out_ref[1, member] = (scale * dot(queried, g, (1, 0))).astype(BF16)


def load_columns(token_refs, held, sems, low, part, heads):
    owners, width = held.shape[1], held.shape[3] // part
    copies = []
    for slot in range(owners):
        start = ((lax.axis_index(HEAD) ^ slot) * heads + low) * width
        cols = pl.ds(pl.multiple_of(start, width), part * width)
        copies.append(
            [
                pltpu.make_async_copy(ref.at[:, cols], held.at[index, slot], sems.at[index, slot])
                for index, ref in enumerate(token_refs)
            ]
        )
        for copy in copies[-1]:
            copy.start()

    def columns_of(slot, member):
        if member == 0:
            for copy in copies[slot]:
                copy.wait()
        return [held[index, slot, :, member * width : (member + 1) * width] for index in range(4)]

    return columns_of


def first_kernel(_, *refs, part, owners):
    decay_refs, token_refs, refs = refs[:owners], refs[owners : owners + 4], refs[owners + 4 :]
    row_ref, col_ref, held, *out_refs, sems = refs
    columns_of = load_columns(token_refs, held, sems, 0, part, row_ref.shape[1])
    prepare(decay_refs, row_ref, col_ref)
    summarize(row_ref, columns_of, out_refs, 0, part)


def later_kernel(row_ref, *refs, low, part):
    token_refs, held, out_refs, sems = refs[:4], refs[4], refs[5:-1], refs[-1]
    columns_of = load_columns(token_refs, held, sems, low, part, row_ref.shape[1])
    summarize(row_ref, columns_of, out_refs, low, part)


def link_layout(owners):
    sizes = dict(near0=owners * owners, near1=owners * owners, after=owners, before=owners, block=1)
    at, total = {}, 0
    for name, size in sizes.items():
        at[name] = total
        total += size
    return sizes, at, -(-total // 8) * 8


def link_kernel(decay_ref, w_ref, *, owners):
    me = lax.axis_index(HEAD)
    sizes, at, length = link_layout(owners)
    heads = decay_ref.shape[0]
    tokens = decay_ref.shape[1] // owners
    index = lax.broadcasted_iota(jnp.int32, (length, 1), 0)
    low = high = keep = jnp.zeros((length, 1), jnp.int32)

    def put(name, low_, high_, keep_):
        nonlocal low, high, keep
        here = (index >= at[name]) & (index < at[name] + sizes[name])
        low = jnp.where(here, low_, low)
        high = jnp.where(here, high_, high)
        keep = jnp.where(here, jnp.where(keep_, 1, 0), keep)

    for side in range(2):
        r = index - at[f"near{side}"]
        to = me ^ lax.div(r, owners)
        of = me ^ lax.rem(r, owners)
        if side == 0:
            put("near0", of, to, of < to)
        else:
            put("near1", to, of, to < of)
    put("after", me ^ (index - at["after"]), owners, index >= 0)
    put("before", -1, me ^ (index - at["before"]), index >= 0)
    put("block", -1, owners, index >= 0)
    spot = lax.broadcasted_iota(jnp.int32, (length, owners * tokens), 1)
    inside = ((spot >= (low + 1) * tokens) & (spot < high * tokens)).astype(BF16)
    total = sum(dot(inside, piece, (1, 1)) for piece in split(decay_ref[...]))
    weight = jnp.where(keep > 0, jnp.exp(-total), 0.0)
    weight = jnp.where(index == at["block"], total, weight)
    for head in range(heads):
        w_ref[head] = jnp.broadcast_to(weight[:, head : head + 1], w_ref.shape[1:])


def extra_rows(part):
    return -(-3 * part // 16) * 16


def log_rows(logs):
    part, lanes = logs.shape
    rows = [piece.astype(F32) for piece in split(logs)]
    rows.append(jnp.zeros((extra_rows(part) - 3 * part, lanes), F32))
    return jnp.concatenate(rows, axis=0).astype(BF16)


def get_logs(ref, part):
    rows = ref[ref.shape[0] - extra_rows(part) :].astype(F32)
    return rows[:part] + rows[part : 2 * part] + rows[2 * part : 3 * part]


def total_kernel(w_ref, *refs, low, part, at, owners):
    out_ref = refs[-1]
    width = out_ref.shape[1]
    for side, name in enumerate(("after", "before")):
        for member in range(part):
            total = 0.0
            for slot, ref in enumerate(refs[:owners]):
                index = at[name] + slot
                total = total + w_ref[low + member, index : index + 1] * ref[side, member].astype(F32)
            rows = slice((side * part + member) * width, (side * part + member + 1) * width)
            out_ref[rows] = total.astype(BF16)
    index = at["block"]
    logs = jnp.concatenate([w_ref[low + m, index : index + 1] for m in range(part)], axis=0)
    out_ref[2 * part * width :] = log_rows(logs)


def pair_kernel(own_ref, other_ref, *out_refs, part):
    far_at = lax.div(lax.axis_index(SEQ), PAIR)
    lead = lax.rem(lax.axis_index(SEQ), PAIR) == 0
    width = own_ref.shape[1]
    own_logs, other_logs = get_logs(own_ref, part), get_logs(other_ref, part)
    over_own, over_other = jnp.exp(-own_logs), jnp.exp(-other_logs)
    weights = (
        (jnp.where(lead, over_other, 1.0), jnp.where(lead, 1.0, over_own)),
        (jnp.where(lead, 1.0, over_other), jnp.where(lead, over_own, 1.0)),
    )
    both_logs = log_rows(own_logs + other_logs)
    for member in range(part):
        both = []
        for side, (own, other) in enumerate(weights):
            rows = slice((side * part + member) * width, (side * part + member + 1) * width)
            both.append(
                own[member : member + 1] * own_ref[rows].astype(F32)
                + other[member : member + 1] * other_ref[rows].astype(F32)
            )
        both = [value.astype(BF16) for value in both]
        for slot, out_ref in enumerate(out_refs):
            onward = (far_at ^ (slot + 1)) > far_at
            rows = slice(member * width, (member + 1) * width)
            out_ref[rows] = jnp.where(onward, both[0], both[1])
    for out_ref in out_refs:
        out_ref[part * width :] = both_logs


def state_kernel(w_ref, *refs, low, part, at, owners, far):
    far_at = lax.div(lax.axis_index(SEQ), PAIR)
    lead = lax.rem(lax.axis_index(SEQ), PAIR) == 0
    ins = refs[:owners]
    other_ref = refs[owners]
    far_refs = refs[owners + 1 : owners + 1 + far]
    out_refs = refs[owners + 1 + far :]
    width = other_ref.shape[1]
    other_logs = get_logs(other_ref, part)
    far_logs = [get_logs(ref, part) for ref in far_refs]
    sources = [far_at ^ (slot + 1) for slot in range(far)]
    for side, enter in enumerate(("before", "after")):
        here = lead if side == 1 else jnp.logical_not(lead)
        gone = jnp.where(here, other_logs, 0.0)
        factors = []
        for source in sources:
            use = source < far_at if side == 0 else source > far_at
            log = gone
            for between, logs in zip(sources, far_logs):
                if side == 0:
                    inside = (between > source) & (between < far_at)
                else:
                    inside = (between < source) & (between > far_at)
                log = log + jnp.where(inside, logs, 0.0)
            factors.append(jnp.where(use, jnp.exp(-log), 0.0))
        for member in range(part):
            rows = slice((side * part + member) * width, (side * part + member + 1) * width)
            base = jnp.where(here, other_ref[rows].astype(F32), 0.0)
            rows = slice(member * width, (member + 1) * width)
            for factor, ref in zip(factors, far_refs):
                base = base + factor[member : member + 1] * ref[rows].astype(F32)
            pieces = [ref[side, member].astype(F32) for ref in ins]
            for slot, out_ref in enumerate(out_refs):
                index = at[enter] + slot
                value = w_ref[low + member, index : index + 1] * base
                for source, piece in enumerate(pieces):
                    if source != slot:
                        index = at[f"near{side}"] + slot * owners + source
                        value = value + w_ref[low + member, index : index + 1] * piece
                out_ref[side, member] = value.astype(BF16)


def inner_parts(row, col, q, k, v, g):
    tokens, width = q.shape
    scale = width ** (-0.5)
    at = lax.broadcasted_iota(jnp.int32, (tokens, tokens), 0)
    by = lax.broadcasted_iota(jnp.int32, (tokens, tokens), 1)
    causal = at >= by
    mask = jnp.where(causal, scale * jnp.exp(-jnp.where(causal, col - row, 0.0)), 0.0)
    scores = (dot(q, k, (1, 1)) * mask).astype(BF16)
    grads = (dot(g, v, (1, 1)) * mask).astype(BF16)
    return (
        dot(scores, v, (1, 0)),
        dot(grads, k, (1, 0)),
        dot(grads, q, (0, 0)),
        dot(scores, g, (0, 0)),
    )


def inner_kernel(row_ref, col_ref, held_ref, *refs, low, part, owners):
    part_refs, scaled_refs = refs[:4], refs[4:]
    _, tokens = row_ref.shape[1:]
    width = part_refs[0].shape[2] // part
    scale = width ** (-0.5)
    for slot in range(owners):
        for member in range(part):
            head = low + member
            here = slice(member * width, (member + 1) * width)
            row = row_ref[slot][head : head + 1, :]
            col = col_ref[slot][:, head : head + 1]
            weight = jnp.exp(-(row[:, tokens - 1 : tokens] - col))
            growth = scale * jnp.exp(-col)
            q, k, v, g = (held_ref[index, slot, :, here] for index in range(4))
            for ref, value in zip(part_refs, inner_parts(row, col, q, k, v, g)):
                ref[slot, :, here] = value
            for ref, rows, factor in zip(scaled_refs, (q, g, v, k), (growth, growth, weight, weight)):
                ref[slot, :, here] = (rows.astype(F32) * factor).astype(BF16)


def result_kernel(*refs, low, part, owners, slots, carried):
    state_refs, refs = refs[: len(slots)], refs[len(slots) :]
    part_refs, scaled_refs, refs = refs[:4], refs[4:8], refs[8 + carried :]
    out_refs, held, sems = refs[:4], *refs[4:]
    width = held.shape[3] // part
    heads = out_refs[0].shape[1] // (owners * width)
    copies = []
    for slot, state_ref in zip(slots, state_refs):
        start = ((lax.axis_index(HEAD) ^ slot) * heads + low) * width
        cols = pl.ds(pl.multiple_of(start, width), part * width)
        for index, out_ref in enumerate(out_refs):
            turned = index in (1, 2)
            for member in range(part):
                here = slice(member * width, (member + 1) * width)
                state = state_ref[index // 2, member]
                value = dot(scaled_refs[index][slot, :, here], state, (1, 1 if turned else 0))
                held[index, slot, :, here] = (part_refs[index][slot, :, here] + value).astype(BF16)
            copy = pltpu.make_async_copy(
                held.at[index, slot], out_ref.at[:, cols], sems.at[index, slot]
            )
            copy.start()
            copies.append(copy)
    for copy in copies:
        copy.wait()


def chunk_sizes(heads):
    return [heads - heads // 2, heads // 2] if heads >= 2 else [heads]


def on_device(query_rows, key_rows, value_rows, out_grad, decay, *, seq_size, owners):
    heads = decay.shape[0]
    tokens, columns = query_rows.shape
    width = columns // (heads * owners)
    chunks = chunk_sizes(heads)
    chunks = [(sum(chunks[:i]), part) for i, part in enumerate(chunks)]
    far = seq_size // PAIR - 1
    _, at, table = link_layout(owners)

    def swap(array, axis, size, offset):
        return lax.ppermute(array, axis, [(i, i ^ offset) for i in range(size)])

    def exchange(arrays):
        return [arrays[0]] + [swap(arrays[slot], HEAD, owners, slot) for slot in range(1, owners)]

    whole = pl.BlockSpec(memory_space=pltpu.VMEM)
    row_shape = jax.ShapeDtypeStruct((owners, heads, tokens), F32)
    col_shape = jax.ShapeDtypeStruct((owners, tokens, heads), F32)
    inputs = [
        pltpu.with_memory_space_constraint(x, pltpu.HBM)
        for x in (query_rows, key_rows, value_rows, out_grad)
    ]

    def state_shapes(part):
        return (jax.ShapeDtypeStruct((2, part, width, width), BF16),) * owners

    def held_shape(part):
        return jax.ShapeDtypeStruct((4, owners, tokens, part * width), BF16)

    def cost(flops, passes, part):
        share = tokens * owners * part * width
        return pl.CostEstimate(flops=flops * share, bytes_accessed=2 * passes * share, transcendentals=0)

    decays = exchange([decay] * owners)
    hbm = pl.BlockSpec(memory_space=pltpu.HBM)
    anywhere = pl.BlockSpec(memory_space=pl.ANY)
    weights = pl.pallas_call(
        functools.partial(link_kernel, owners=owners),
        out_shape=jax.ShapeDtypeStruct((heads, table, width), F32),
        in_specs=[whole],
        out_specs=whole,
        cost_estimate=pl.CostEstimate(flops=0, bytes_accessed=24 * tokens * columns, transcendentals=0),
        compiler_params=params(),
        name="link",
    )(decay)
    part = chunks[0][1]
    rows, cols, *first = pl.pallas_call(
        functools.partial(first_kernel, part=part, owners=owners),
        out_shape=(row_shape, col_shape, held_shape(part)) + state_shapes(part),
        in_specs=[anywhere] + [whole] * owners + [hbm] * 4,
        out_specs=(whole,) * (3 + owners),
        scratch_shapes=[pltpu.SemaphoreType.DMA((4, owners))],
        cost_estimate=cost(4 * width, 4, part),
        compiler_params=params(),
        name="first",
    )(weights, *decays, *inputs)
    summaries = [first]
    for low, part in chunks[1:]:
        summary_call = pl.pallas_call(
            functools.partial(later_kernel, low=low, part=part),
            out_shape=(held_shape(part),) + state_shapes(part),
            in_specs=[whole] + [hbm] * 4,
            out_specs=(whole,) * (1 + owners),
            scratch_shapes=[pltpu.SemaphoreType.DMA((4, owners))],
            cost_estimate=cost(4 * width, 4, part),
            compiler_params=params(),
        )
        summaries.append(summary_call(rows, *inputs))

    outs = None
    for chunk, (low, part) in enumerate(chunks):
        total_shape = jax.ShapeDtypeStruct((2 * part * width + extra_rows(part), width), BF16)
        far_shape = jax.ShapeDtypeStruct((part * width + extra_rows(part), width), BF16)
        part_shape = jax.ShapeDtypeStruct((owners, tokens, part * width), F32)
        scaled_shape = jax.ShapeDtypeStruct((owners, tokens, part * width), BF16)
        held, *own = summaries[chunk]
        here = exchange(own)
        total_call = pl.pallas_call(
            functools.partial(total_kernel, low=low, part=part, at=at, owners=owners),
            out_shape=total_shape,
            in_specs=[whole] * (owners + 1),
            out_specs=whole,
            compiler_params=params(),
        )
        total = total_call(weights, *here)
        other = swap(total, SEQ, seq_size, 1)
        pair_call = pl.pallas_call(
            functools.partial(pair_kernel, part=part),
            out_shape=(far_shape,) * far,
            in_specs=[whole, whole],
            out_specs=(whole,) * far,
            compiler_params=params(),
        )
        sent = pair_call(total, other)
        heard = [swap(array, SEQ, seq_size, PAIR * (slot + 1)) for slot, array in enumerate(sent)]
        state_call = pl.pallas_call(
            functools.partial(
                state_kernel, low=low, part=part, at=at, owners=owners, far=far
            ),
            out_shape=state_shapes(part),
            in_specs=[whole] * (owners + far + 2),
            out_specs=(whole,) * owners,
            compiler_params=params(),
        )
        states = state_call(weights, *here, other, *heard)
        states = exchange(states)
        inner_call = pl.pallas_call(
            functools.partial(inner_kernel, low=low, part=part, owners=owners),
            out_shape=(part_shape,) * 4 + (scaled_shape,) * 4,
            in_specs=[whole] * 3,
            out_specs=(whole,) * 8,
            cost_estimate=cost(12 * tokens, 12, part),
            compiler_params=params(),
        )
        parts = inner_call(rows, cols, held)
        groups = [range(owners)]
        if chunk == len(chunks) - 1:
            half = owners // 2
            groups = [(0,), (half,), [slot for slot in range(1, owners) if slot != half]]
        for slots in groups:
            carried = 0 if outs is None else 4
            first_carried = 8 + len(slots)
            outs = pl.pallas_call(
                functools.partial(
                    result_kernel,
                    low=low,
                    part=part,
                    owners=owners,
                    slots=tuple(slots),
                    carried=carried,
                ),
                out_shape=(jax.ShapeDtypeStruct((tokens, columns), BF16),) * 4,
                in_specs=[whole] * (8 + len(slots)) + [hbm] * carried,
                out_specs=(hbm,) * 4,
                scratch_shapes=[
                    pltpu.VMEM((4, owners, tokens, part * width), BF16),
                    pltpu.SemaphoreType.DMA((4, owners)),
                ],
                input_output_aliases={first_carried + i: i for i in range(carried)},
                cost_estimate=cost(8 * width, 8, part),
                compiler_params=params(),
            )(*[states[slot] for slot in slots], *parts, *(outs or ()))
    return tuple(outs)


def solution(mesh):
    spec = P((SEQ, HEAD), None)

    def body(*args):
        return on_device(*args, seq_size=mesh.shape[SEQ], owners=mesh.shape[HEAD])

    return jax.shard_map(
        body,
        mesh=mesh,
        in_specs=(spec, spec, spec, spec, P(HEAD, SEQ)),
        out_specs=(spec, spec, spec, spec),
        check_vma=False,
    )
```
